32 devices in a mesh: bx: 4 (over y, x), by: 8 (over z, core).
Axes of the slice: x: 2, y: 2, z: 4, core: 2. Of those that a mesh axis runs over, the one named last changes fastest.
Arguments:
- terminal_value: float32 [64, 128, 256], P('bx', 'by'), may hold values from -3 to 3
- density: float32 [64, 128, 256], P('bx', 'by')
- potential: float32 [64, 128, 256], P('bx', 'by'), may hold values from -5 to 5
- heights: int32 [64, 128], P('bx', 'by'), may hold values from 0 to 64
Outputs:
- value_field: float32 [64, 128, 256], P('bx', 'by')
- density_next: float32 [64, 128, 256], P('bx', 'by')
The draws below stay inside these ranges and needn't reach their ends.
All inputs are finite; a program needn't handle non-finite values.
Results may differ from the reference program's by a relative error of at most 0.0001.
Values sent between devices are 32-bit elements; how exact they have to be, the bound alone decides.
A program may use at most 64 MiB of HBM per device.

```python
import jax
import jax.numpy as jnp
from jax import lax

NZ = 256
ITERS = 3
NX = 64
NY = 128


def draw_density(key, part):
    shape = (NX, NY, NZ)
    first = lax.broadcasted_iota(jnp.float32, shape, 0) / NX
    second = lax.broadcasted_iota(jnp.float32, shape, 1) / NY
    ramp = (1.0 + 2.0 * first) * (1.0 + 2.0 * second) / 4.0
    rough = jax.random.uniform(key, shape, jnp.float32, 0.25, 1.75)
    return (ramp * rough).astype(jnp.float32)


def touch_ends(values, rng, least, largest):
    longest = values.shape.index(max(values.shape))
    spots = []
    for shift in (0, 1):
        where = [jax.random.randint(jax.random.fold_in(rng, axis), (), 0, length) for axis, length in enumerate(values.shape)]
        where[longest] = (where[longest] + shift) % values.shape[longest]
        spots.append(tuple(where))
    return values.at[spots[0]].set(least).at[spots[1]].set(largest)


def level_of(stream_key, extent, pieces, smallest, high):
    gain = 1.0
    for dim, shards_of in pieces:
        steps = jax.random.uniform(jax.random.fold_in(jax.random.fold_in(stream_key, 6), dim), (shards_of,), jnp.float32, smallest / len(pieces), high / len(pieces))
        gain = gain * jnp.repeat(jnp.exp(steps), extent[dim] // shards_of).reshape((-1,) + (1,) * (len(extent) - 1 - dim))
    return gain


def scatter_about(own_key, shape, spread, bound, cuts=(), kind=jnp.bfloat16):
    array = jax.random.normal(own_key, shape, jnp.float32) * spread
    if len(cuts) > 0:
        array = level_of(own_key, shape, cuts, -0.22, 0.18) * array
    return jnp.clip(array, min=-bound, max=bound).astype(kind)


def setup_inputs(seed: int = 0) -> dict:
    arg_keys = jax.random.split(jax.random.key(seed), 5)
    terminal_value = scatter_about(arg_keys[0], (NX, NY, NZ), 0.5, 3.0, ((0, 4), (1, 8)), jnp.float32)
    density = draw_density(jax.random.fold_in(arg_keys[4], 71), 0)
    potential = scatter_about(arg_keys[2], (NX, NY, NZ), 1.0, 5.0, ((0, 4), (1, 8)), jnp.float32)
    heights = touch_ends(jax.random.randint(arg_keys[3], (NX, NY), 0, NZ // 4 + 1), jax.random.fold_in(arg_keys[3], 1), 0, (NZ // 4 + 1) - 1).astype(jnp.int32)
    return {"terminal_value": terminal_value, "density": density, "potential": potential, "heights": heights}


DT_HJB = 0.5
NU_HJB = 0.25
COUPLE = 0.5
PENALTY = 2.0
DT_FP = 0.25
DIFFUSE = 1.0
ABSORB = 4.0


def neighbours(padded):
    full = jnp.pad(padded, ((0, 0), (0, 0), (1, 1)))
    centre = full[1:-1, 1:-1, 1:-1]
    pairs = [(full[2:, 1:-1, 1:-1], full[:-2, 1:-1, 1:-1]),
             (full[1:-1, 2:, 1:-1], full[1:-1, :-2, 1:-1]),
             (full[1:-1, 1:-1, 2:], full[1:-1, 1:-1, :-2])]
    return centre, pairs


def hjb_update(padded, cost):
    centre, pairs = neighbours(padded)
    laplace = -6.0 * centre
    hamilton = jnp.zeros_like(centre)
    for upper, lower in pairs:
        laplace = laplace + upper + lower
        hamilton = hamilton + jnp.square(jnp.maximum(centre - lower, 0.0)) + jnp.square(jnp.minimum(upper - centre, 0.0))
    return centre + DT_HJB * (NU_HJB * laplace - 0.5 * hamilton + cost)


def transport(mass_pad, value_pad):
    mass, mass_pairs = neighbours(mass_pad)
    value, value_pairs = neighbours(value_pad)
    divergence = jnp.zeros_like(mass)
    for mass_side, value_side in zip(mass_pairs, value_pairs):
        mass_up, mass_low = mass_side
        value_up, value_low = value_side
        speed_up = value - value_up
        flux_up = jnp.maximum(speed_up, 0.0) * mass + jnp.minimum(speed_up, 0.0) * mass_up
        speed_low = value_low - value
        flux_low = jnp.maximum(speed_low, 0.0) * mass_low + jnp.minimum(speed_low, 0.0) * mass
        divergence = divergence + (flux_up - flux_low)
    return mass - DT_FP * divergence


def operate(padded, diagonal):
    centre, pairs = neighbours(padded)
    total = jnp.zeros_like(centre)
    for upper, lower in pairs:
        total = total + upper + lower
    return diagonal * centre - DIFFUSE * total


def pad_plane(field):
    return jnp.pad(field, ((1, 1), (1, 1), (0, 0)))


def reference(terminal_value, density, potential, heights):
    levels = lax.broadcasted_iota(jnp.int32, (1, 1, NZ), 2)
    blocked = (levels < heights[:, :, None]).astype(jnp.float32)
    cost = potential + COUPLE * density + PENALTY * blocked
    value_mid = hjb_update(pad_plane(terminal_value), cost)
    value_field = hjb_update(pad_plane(value_mid), cost)
    target = transport(pad_plane(density), pad_plane(value_field))
    diagonal = 1.0 + 6.0 * DIFFUSE + ABSORB * blocked
    solution = target
    residual = target - operate(pad_plane(target), diagonal)
    direction = residual
    norm_now = jnp.sum(residual * residual)
    for iteration in range(ITERS):
        image = operate(pad_plane(direction), diagonal)
        alpha = norm_now / jnp.sum(direction * image)
        solution = solution + alpha * direction
        residual = residual - alpha * image
        norm_next = jnp.sum(residual * residual)
        direction = residual + (norm_next / norm_now) * direction
        norm_now = norm_next
    return value_field, solution
```

```python
import functools

import jax
import jax.numpy as jnp
from jax import lax
from jax.experimental import pallas as pl
from jax.experimental.pallas import tpu as pltpu
from jax.sharding import PartitionSpec as P_

DT_HJB = 0.5
NU_HJB = 0.25
COUPLE = 0.5
PENALTY = 2.0
DT_FP = 0.25
ABSORB = 4.0
SHIFT = 7.0

X0 = 4
HALO = 8
VMEM_LIMIT = 56_000_000
MESH = pl.DeviceIdType.MESH


class Link:
    def __init__(self, src, dst, send, recv, device, side):
        self.copy = pltpu.make_async_remote_copy(
            src_ref=src, dst_ref=dst, send_sem=send, recv_sem=recv,
            device_id=device, device_id_type=MESH)
        self.side = side


def kernel(nbx, nby, t_in, m_in, p_in, h_in, v_out, s_out,
           T, P, D, C, M, V, G, B1, Q, D4, HB, PA, PB,
           ssem, rsem, asend, arecv, bsend, brecv, lsem):
    nx, ny, nz = v_out.shape
    bx, by = lax.axis_index("bx"), lax.axis_index("by")
    XE, YE, X1 = nx + 2 * X0, ny + HALO, X0 + nx
    has = {-1: bx > 0, 1: bx < nbx - 1}
    hasy = {-1: by > 0, 1: by < nby - 1}

    def exists(dx, dy):
        if dx == 0:
            return hasy[dy]
        if dy == 0:
            return has[dx]
        return has[dx] & hasy[dy]

    sides = [(dx, dy) for dx in (-1, 0, 1) for dy in (-1, 0, 1) if (dx, dy) != (0, 0)]
    diagonals = [d for d in sides if d[0] and d[1]]
    there = {d: exists(*d) for d in sides}

    barrier = pltpu.get_barrier_semaphore()
    for k in range(1, nby):
        pl.semaphore_signal(barrier, inc=1, device_id=(bx, lax.rem(by + k, nby)), device_id_type=MESH)
    for k in range(1, nbx):
        pl.semaphore_signal(barrier, inc=1, device_id=(lax.rem(bx + k, nbx), by), device_id_type=MESH)
    greeted = (nby - 1) + (nbx - 1)
    for d in diagonals:
        @pl.when(there[d])
        def _():
            pl.semaphore_signal(barrier, inc=1, device_id=(bx + d[0], by + d[1]), device_id_type=MESH)
        greeted = greeted + there[d].astype(jnp.int32)

    rows = pl.ds(0, ny)
    beyond = pl.ds(ny, HALO)
    own = pl.ds(X0, nx)
    loads = [
        pltpu.make_async_copy(h_in, HB.at[1, 1], lsem.at[3]),
        pltpu.make_async_copy(m_in, D.at[own, rows], lsem.at[1]),
        pltpu.make_async_copy(p_in, P.at[own, rows], lsem.at[2]),
        pltpu.make_async_copy(t_in, T.at[own, rows], lsem.at[0]),
    ]
    for c in loads:
        c.start()

    count = [0]

    def link(src, dst, side):
        i = count[0]
        count[0] += 1
        return Link(src, dst, ssem.at[i], rsem.at[i], (bx + side[0], by + side[1]), side)

    def by_side(links):
        groups = {}
        for c in links:
            groups.setdefault(c.side, []).append(c)
        return groups

    def start(links):
        for side, group in by_side(links).items():
            @pl.when(there[side])
            def _():
                for c in group:
                    c.copy.start()

    def wait_recv(links):
        for side, group in by_side(links).items():
            @pl.when(there[(-side[0], -side[1])])
            def _():
                for c in group:
                    c.copy.wait_recv()

    def wait_send(links):
        for side, group in by_side(links).items():
            @pl.when(there[side])
            def _():
                for c in group:
                    c.copy.wait_send()

    def x_from(d, w):
        return pl.ds(nx - w, w) if d > 0 else pl.ds(0, w)

    def x_to(d, w):
        return pl.ds(X0 - w, w) if d > 0 else pl.ds(X1, w)

    def y_from(d, w):
        return pl.ds(ny - w, w) if d > 0 else pl.ds(0, w)

    def y_to(d, w):
        return pl.ds(YE - w, w) if d > 0 else pl.ds(ny, w)

    def input_link(src, dst, side, wx, wy):
        dx, dy = side
        xs = (x_from(dx, wx), x_to(dx, wx)) if dx else (pl.ds(0, nx), own)
        ys = (y_from(dy, wy), y_to(dy, wy)) if dy else (rows, rows)
        return link(src.at[xs[0], ys[0]], dst.at[xs[1], ys[1]], side)

    def field_link(side, wx, wy):
        dx, dy = side
        xs = (pl.ds(X1 - wx, wx), x_to(dx, wx)) if dx > 0 else (pl.ds(X0, wx), x_to(dx, wx))
        ys = (y_from(dy, wy), y_to(dy, wy)) if dy else (rows, rows)
        return link(G.at[xs[0], ys[0]], G.at[xs[1], ys[1]], side)

    def strips(planes):
        return [link(G.at[planes, y_from(d, w)], G.at[planes, y_to(d, w)], (0, d)) for d, w in ((1, 3), (-1, 4))]

    def heights_link(side):
        return link(h_in, HB.at[1 - side[0], 1 - side[1]], side)

    flat = [(-1, 0), (1, 0)]
    tall = [(0, -1), (0, 1)]
    hy = [heights_link(d) for d in tall]
    hx = [heights_link(d) for d in flat + diagonals]
    ty = [input_link(a, b, d, 0, w) for a, b, w in ((t_in, T, 3), (p_in, P, 2), (m_in, D, 2)) for d in tall]
    tx = [input_link(a, b, d, w, 0) for a, b, w in ((t_in, T, 3), (p_in, P, 2), (m_in, D, 2)) for d in flat]
    tc = [input_link(a, b, d, w, w) for a, b, w in ((t_in, T, 2), (p_in, P, 1), (m_in, D, 1)) for d in diagonals]

    def zero_planes(lo):
        for buf in (T, D, G):
            buf[pl.ds(lo, X0)] = jnp.zeros((X0, YE, nz), jnp.float32)

    def zero_rows(lo):
        for buf in (T, D, G):
            buf[:, pl.ds(lo, 4), :] = jnp.zeros((XE, 4, nz), jnp.float32)

    pl.when(jnp.logical_not(has[-1]))(lambda: zero_planes(0))
    pl.when(jnp.logical_not(has[1]))(lambda: zero_planes(X1))
    pl.when(jnp.logical_not(hasy[1]))(lambda: zero_rows(ny))
    pl.when(jnp.logical_not(hasy[-1]))(lambda: zero_rows(ny + 4))

    pl.semaphore_wait(barrier, greeted)
    start(hx + hy + ty + tx + tc)

    def column(side, part, x, n, first):
        line = HB[side, part, pl.ds(x, 1), :].astype(jnp.float32)
        lanes = lax.broadcasted_iota(jnp.int32, (n, ny), 1)
        subs = lax.broadcasted_iota(jnp.int32, (n, ny), 0) + first
        return jnp.sum(jnp.where(lanes == subs, line, 0.0), axis=1, keepdims=True)

    def level_mask(col, high):
        level = lax.broadcasted_iota(jnp.int32, (col.shape[0], nz), 1).astype(jnp.float32)
        return jnp.where(level < col, high, 0.0)

    def obstacles(side, x, i):
        D4[i, rows, :] = level_mask(column(side, 1, x, ny, 0), ABSORB)

    def beyond_obstacles(side, x, i):
        col = jnp.where(lax.broadcasted_iota(jnp.int32, (8, 1), 0) < 4,
                        column(side, 2, x, 8, 0), column(side, 0, x, 8, ny - 8))
        D4[i, beyond, :] = level_mask(col, ABSORB)

    def cost(i, part):
        C[i, part, :] = P[i, part, :] + COUPLE * D[i, part, :] + (PENALTY / ABSORB) * D4[i, part, :]

    row8 = lax.broadcasted_iota(jnp.int32, (8, nz), 0)
    keep = (row8 >= jnp.where(hasy[1], 0, 4)) & (row8 < jnp.where(hasy[-1], 8, 4))

    def loop(lo, hi, f):
        step = 4 if (hi - lo) % 4 == 0 else 1

        @pl.loop(0, (hi - lo) // step)
        def _(j):
            for k in range(step):
                f(lo + step * j + k)

    def pairs(lo, hi, value, store):
        @pl.loop(0, (hi - lo) // 2)
        def _(j):
            i = lo + 2 * j
            a, b = value(i), value(i + 1)
            store(i, a)
            store(i + 1, b)

    def each(planes, value, store):
        for i in planes:
            store(i, value(i))

    def ends(k, e, value, store):
        @pl.loop(0, k + e)
        def _(j):
            i, n = X0 - k + j, X1 - e + j
            a, b = value(i), value(n)
            store(i, a)
            store(n, b)

    def clear(buf, low, high):
        def zero(lo, k):
            buf[pl.ds(lo, k)] = jnp.zeros((k, YE, nz), jnp.float32)
        if low:
            pl.when(jnp.logical_not(has[-1]))(lambda: zero(X0 - low, low))
        if high:
            pl.when(jnp.logical_not(has[1]))(lambda: zero(X1, high))

    lane = lax.broadcasted_iota(jnp.int32, (YE, 128), 1)

    def z_up(v):
        n = v.shape[0]
        tiles = [pltpu.roll(v[:, j:j + 128], 127, 1) for j in range(0, nz, 128)]
        tiles.append(jnp.zeros_like(tiles[0]))
        return jnp.concatenate([jnp.where(lane[:n] == 127, b, a) for a, b in zip(tiles, tiles[1:])], axis=1)

    def z_low(v, edge=None):
        n = v.shape[0]
        tiles = [jnp.zeros((n, 128), jnp.float32) if edge is None else edge]
        tiles += [pltpu.roll(v[:, j:j + 128], 1, 1) for j in range(0, nz, 128)]
        return jnp.concatenate([jnp.where(lane[:n] == 0, a, b) for a, b in zip(tiles, tiles[1:])], axis=1)

    def put(dst, i, v):
        dst[i, rows, :] = v[:ny]
        dst[i, beyond, :] = jnp.where(keep, v[ny:], 0.0)

    def hjb(src):
        def f(i):
            v = src[i]
            lap = -6.0 * v
            ham = jnp.zeros_like(v)
            for u, l in ((src[i + 1], src[i - 1]), (pltpu.roll(v, YE - 1, 0), pltpu.roll(v, 1, 0)),
                         (z_up(v), z_low(v))):
                lap = lap + (u + l)
                ham = ham + jnp.square(jnp.maximum(v - l, 0.0)) + jnp.square(jnp.minimum(u - v, 0.0))
            return v + DT_HJB * (NU_HJB * lap - 0.5 * ham + C[i])
        return f

    def put_mid(i, v):
        put(M, i, v)

    def put_halo(i, v):
        put(V, i, v)

    def put_value(i, v):
        put(V, i, v)
        v_out[i - X0] = v[:ny]

    def flux(v, vu, m, mu):
        s = v - vu
        return jnp.maximum(s, 0.0) * m + jnp.minimum(s, 0.0) * mu

    def x_flux(i):
        return flux(V[i, rows, :], V[i + 1, rows, :], D[i, rows, :], D[i + 1, rows, :])

    def transport(starts, n):
        def one(i, before):
            v, m = V[i], D[i]
            fy = flux(v, pltpu.roll(v, YE - 1, 0), m, pltpu.roll(m, YE - 1, 0))
            ly = pltpu.roll(fy, 1, 0)[:ny]
            v, m = v[:ny], m[:ny]
            fz = flux(v, z_up(v), m, z_up(m))
            lz = z_low(fz, jnp.minimum(-v[:, :128], 0.0) * m[:, :128])
            fx = x_flux(i)
            return fx, m - DT_FP * ((fx - before) + (fy[:ny] - ly) + (fz - lz))

        def f(j, before):
            done = [one(lo + j, b) for lo, b in zip(starts, before)]
            for lo, d in zip(starts, done):
                G[lo + j, rows, :] = d[1]
            return tuple(d[0] for d in done)
        lax.fori_loop(0, n, f, tuple(x_flux(lo - 1) for lo in starts))

    half = nx // 2
    for c in loads[:3]:
        c.wait()

    def own_cost(i):
        obstacles(1, i - X0, i)
        cost(i, rows)

    loop(X0, X1, own_cost)
    wait_recv(hy + ty)

    def beyond_cost(i):
        beyond_obstacles(1, i - X0, i)
        cost(i, beyond)

    loop(X0, X1, beyond_cost)
    loads[3].wait()
    pairs(X0 + 1, X1 - 1, hjb(T), put_mid)
    pairs(X0 + 2, X1 - 2, hjb(M), put_value)
    transport((X0 + 3, X0 + half), half - 3)
    gi = strips(pl.ds(X0 + 3, nx - 6)) + [link(G.at[X0 + 3, rows], G.at[X1 + 3, rows], (-1, 0))]
    start(gi)

    wait_recv(hx)

    def halo_obstacles(side, x, i):
        obstacles(side, x, i)
        beyond_obstacles(side, x, i)

    for j in range(2):
        halo_obstacles(0, nx - 2 + j, X0 - 2 + j)
    for j in range(3):
        halo_obstacles(2, j, X1 + j)

    wait_recv(tx + tc)
    for i in (X0 - 2, X0 - 1, X1, X1 + 1):
        cost(i, pl.ds(0, YE))
    ends(2, 1, hjb(T), put_mid)
    clear(M, 2, 2)
    ends(0, 2, hjb(M), put_value)
    for i in (X0 - 1, X1):
        put_halo(i, hjb(M)(i))
    clear(V, 1, 1)
    transport((X0, X1 - 3), 3)

    gx = [field_link(d, 3, 0) for d in flat] + [field_link(d, 3, 3) for d in diagonals]
    gy = strips(pl.ds(X0, 3)) + strips(pl.ds(X1 - 3, 3))
    start(gx + gy)

    def shifted(src):
        def f(i):
            v = src[i]
            return D4[i] * v - ((src[i + 1] + src[i - 1]) + (pltpu.roll(v, YE - 1, 0) + pltpu.roll(v, 1, 0))
                                + (z_up(v) + z_low(v)))
        return f

    R = M

    def residual(i):
        return (1.0 - SHIFT) * G[i] - shifted(G)(i)

    def into(dst):
        return lambda i, v: put(dst, i, v)

    def moments(i, sums):
        r, b = R[i, rows, :], B1[i, rows, :]
        full = Q[i]
        yu = pltpu.roll(full, YE - 1, 0)[:ny]
        q = full[:ny]
        image = D4[i, rows, :] * q - 2.0 * (Q[i + 1, rows, :] + yu + z_up(q))
        terms = (r * r, r * b, b * b, b * q, q * q, q * image)

        def fold(a):
            a = a.reshape(ny // 8, 8, nz).sum(axis=0)
            return sum(a[:, j:j + 128] for j in range(0, nz, 128))

        return tuple(s + fold(a) for s, a in zip(sums, terms))

    wait_recv(gi[:2])
    pairs(X0 + 4, X1 - 4, residual, into(R))
    wait_recv(gy)
    ends(-1, 4, residual, into(R))
    pairs(X0 + 2, X1 - 2, shifted(R), into(B1))
    pairs(X0 + 3, X1 - 3, shifted(B1), into(Q))

    def two(j, sums):
        return moments(X0 + 4 + 2 * j, moments(X0 + 3 + 2 * j, sums))

    zero = jnp.zeros((8, 128), jnp.float32)
    sums = lax.fori_loop(0, (nx - 8) // 2, two, (zero,) * 6)

    wait_recv(gx + gi[2:])
    ends(2, 1, residual, into(R))
    into(R)(X1 + 2, residual(X1 + 2))
    clear(R, 2, 3)
    ends(1, 2, shifted(R), into(B1))
    into(B1)(X1 + 1, shifted(R)(X1 + 1))
    clear(B1, 1, 2)
    ends(0, 3, shifted(B1), into(Q))
    into(Q)(X1, shifted(B1)(X1))
    clear(Q, 0, 1)

    def rest(j, sums):
        for k in (2 * j, 2 * j + 1):
            sums = moments(X0 + k + jnp.where(k >= 3, nx - 8, 0), sums)
        return sums

    sums = lax.fori_loop(0, 4, rest, sums)
    tile_row = lax.broadcasted_iota(jnp.int32, (8, 128), 0)
    tile = zero
    for k, s in enumerate(sums):
        tile = jnp.where(tile_row == k, jnp.sum(s, axis=0, keepdims=True), tile)
    tile = jnp.sum(tile, axis=1, keepdims=True)
    tile = jnp.sum(jnp.where(tile_row == lane[:8], tile, 0.0), axis=0, keepdims=True)

    def all_sum(slots, value, n, me, device, send, recv):
        slots[me] = value
        copies = []
        for k in range(1, n):
            c = pltpu.make_async_remote_copy(
                src_ref=slots.at[me], dst_ref=slots.at[me], send_sem=send.at[k - 1], recv_sem=recv.at[k - 1],
                device_id=device(lax.rem(me + k, n)), device_id_type=MESH)
            c.start()
            copies.append(c)
        for k in range(1, n):
            source = lax.rem(me + n - k, n)
            pltpu.make_async_remote_copy(
                src_ref=slots.at[source], dst_ref=slots.at[source], send_sem=send.at[k - 1], recv_sem=recv.at[k - 1],
                device_id=device(source), device_id_type=MESH).wait_recv()
        return copies, jnp.sum(slots[...], axis=0)

    ca, tile = all_sum(PA, tile, nby, by, lambda j: (bx, j), asend, arecv)
    cb, tile = all_sum(PB, tile, nbx, bx, lambda j: (j, by), bsend, brecv)
    nu = [jnp.broadcast_to(tile[:, k:k + 1], (1, 128)) for k in range(6)]

    def dot(p, q, s):
        total = 0.0
        for i, a in enumerate(p):
            for j, b in enumerate(q):
                total = total + a * b * nu[i + j + s]
        return total

    def energy(p):
        return SHIFT * dot(p, p, 0) + dot(p, p, 1)

    def step_of(rr, p):
        return jnp.clip(rr / energy(p), 1.0 / 17.0, 1.0)

    one = jnp.ones_like(nu[0])
    rr = nu[0]
    p, r = (one,), (one,)
    x = None
    for it in range(3):
        a = step_of(rr, p)
        x = [a * c for c in p] if x is None else [x[j] + a * p[j] if j < len(x) else a * p[j] for j in range(len(p))]
        if it == 2:
            break
        image = [SHIFT * c for c in p] + [jnp.zeros_like(one)]
        for j, c in enumerate(p):
            image[j + 1] = image[j + 1] + c
        r = tuple((r[j] if j < len(r) else 0.0) - a * image[j] for j in range(len(image)))
        new = jnp.maximum(dot(r, r, 0), 0.0)
        beta = new / rr
        p = tuple(r[j] + (beta * p[j] if j < len(p) else 0.0) for j in range(len(r)))
        rr = new
    x = [jnp.concatenate([c] * (nz // 128), axis=1) for c in x]

    def finish(i):
        s_out[i - X0] = G[i, rows, :] + x[0] * R[i, rows, :] + x[1] * B1[i, rows, :] + x[2] * Q[i, rows, :]

    loop(X0, X1, finish)

    wait_send(hx + hy + ty + tx + tc + gi + gx + gy)
    for c in ca + cb:
        c.wait_send()


LINKS = 56


def write(v, s, v_out, s_out, sem):
    copies = [pltpu.make_async_copy(v, v_out, sem.at[0]), pltpu.make_async_copy(s, s_out, sem.at[1])]
    for c in copies:
        c.start()
    for c in copies:
        c.wait()


def per_device(nbx, nby, t, m, p, h):
    nx, ny, nz = t.shape
    ext = pltpu.VMEM((nx + 2 * X0, ny + HALO, nz), jnp.float32)
    out = jax.ShapeDtypeStruct(t.shape, jnp.float32)
    v, s = pl.pallas_call(
        functools.partial(kernel, nbx, nby),
        out_shape=(out, out),
        in_specs=[pl.BlockSpec(memory_space=pl.ANY)] * 4,
        out_specs=(pl.BlockSpec(memory_space=pltpu.VMEM),) * 2,
        scratch_shapes=[ext] * 10 + [
            pltpu.VMEM((3, 3, nx, ny), jnp.int32),
            pltpu.VMEM((nby, 1, 128), jnp.float32), pltpu.VMEM((nbx, 1, 128), jnp.float32),
            pltpu.SemaphoreType.DMA((LINKS,)), pltpu.SemaphoreType.DMA((LINKS,)),
            pltpu.SemaphoreType.DMA((nby - 1,)), pltpu.SemaphoreType.DMA((nby - 1,)),
            pltpu.SemaphoreType.DMA((nbx - 1,)), pltpu.SemaphoreType.DMA((nbx - 1,)),
            pltpu.SemaphoreType.DMA((4,)),
        ],
        compiler_params=pltpu.CompilerParams(collective_id=0, has_side_effects=True, vmem_limit_bytes=VMEM_LIMIT),
        name="mean_field_step",
    )(*(pltpu.with_memory_space_constraint(a, pltpu.HBM) for a in (t, m, p, h)))
    return pl.pallas_call(
        write,
        out_shape=(out, out),
        in_specs=[pl.BlockSpec(memory_space=pltpu.VMEM)] * 2,
        out_specs=(pl.BlockSpec(memory_space=pl.ANY),) * 2,
        scratch_shapes=[pltpu.SemaphoreType.DMA((2,))],
        compiler_params=pltpu.CompilerParams(vmem_limit_bytes=4_000_000),
        name="write",
    )(v, s)


def solution(mesh):
    cells, plane = P_("bx", "by", None), P_("bx", "by")
    return jax.shard_map(
        functools.partial(per_device, mesh.shape["bx"], mesh.shape["by"]),
        mesh=mesh, in_specs=(cells, cells, cells, plane), out_specs=(cells, cells), check_vma=False)
```

```python
import functools

import jax
import jax.numpy as jnp
from jax import lax
from jax.experimental import pallas as pl
from jax.experimental.pallas import tpu as pltpu
from jax.sharding import PartitionSpec as P_

DT_HJB = 0.5
NU_HJB = 0.25
COUPLE = 0.5
PENALTY = 2.0
DT_FP = 0.25
ABSORB = 4.0
SHIFT = 7.0

X0 = 4
HALO = 8
ONE_STAGE = 64
VMEM_LIMIT = 56_000_000
MESH = pl.DeviceIdType.MESH


class Link:
    def __init__(self, src, dst, send, recv, device, side, relay=None):
        self.copy = pltpu.make_async_remote_copy(
            src_ref=src, dst_ref=dst, send_sem=send, recv_sem=recv,
            device_id=device, device_id_type=MESH)
        self.side = side
        self.relay = relay


def kernel(nbx, nby, t_in, m_in, p_in, h_in, v_out, s_out,
           T, C, D, M, V, G, B1, Q, D4, POT, RB, HB, PA, PB,
           ssem, rsem, asend, arecv, bsend, brecv, lsem):
    nx, ny, nz = v_out.shape
    bx, by = lax.axis_index("bx"), lax.axis_index("by")
    XE, YE, X1 = nx + 2 * X0, ny + HALO, X0 + nx
    has = {-1: bx > 0, 1: bx < nbx - 1}
    hasy = {-1: by > 0, 1: by < nby - 1}

    def exists(dx, dy):
        if dx == 0:
            return hasy[dy]
        if dy == 0:
            return has[dx]
        return has[dx] & hasy[dy]

    sides = [(dx, dy) for dx in (-1, 0, 1) for dy in (-1, 0, 1) if (dx, dy) != (0, 0)]
    diagonals = [d for d in sides if d[0] and d[1]]
    there = {d: exists(*d) for d in sides}

    barrier = pltpu.get_barrier_semaphore()
    whole = nbx * nby <= ONE_STAGE
    lines = [(0, j) for j in range(1, nby)] + [(i, 0) for i in range(1, nbx)]
    peers = [(i, j) for j in range(nby) for i in range(nbx) if (i, j) != (0, 0)] if whole else lines

    def peer(i, j):
        return lax.rem(bx + i, nbx), lax.rem(by + j, nby)

    for d in peers:
        pl.semaphore_signal(barrier, inc=1, device_id=peer(*d), device_id_type=MESH)
    greeted = len(peers)
    if not whole:
        for d in diagonals:
            @pl.when(there[d])
            def _():
                pl.semaphore_signal(barrier, inc=1, device_id=(bx + d[0], by + d[1]), device_id_type=MESH)
            greeted = greeted + there[d].astype(jnp.int32)

    rows = pl.ds(0, ny)
    beyond = pl.ds(ny, HALO)
    own = pl.ds(X0, nx)
    loads = [
        pltpu.make_async_copy(h_in, HB.at[1, 1], lsem.at[3]),
        pltpu.make_async_copy(m_in, D.at[own, rows], lsem.at[1]),
        pltpu.make_async_copy(p_in, POT, lsem.at[2]),
        pltpu.make_async_copy(t_in, T.at[own, rows], lsem.at[0]),
    ]
    for c in loads:
        c.start()

    count = [0]

    def link(src, dst, side, relay=None):
        i = count[0]
        count[0] += 1
        return Link(src, dst, ssem.at[i], rsem.at[i], (bx + side[0], by + side[1]), side, relay)

    def grouped(links, sends):
        groups = {}
        for c in links:
            groups.setdefault((c.side, c.relay), []).append(c)
        for (side, relay), group in groups.items():
            if relay is not None:
                here = bx == relay[0 if sends else 1]
            else:
                here = there[side] if sends else there[(-side[0], -side[1])]
            yield here, group

    def start(links):
        for here, group in grouped(links, True):
            @pl.when(here)
            def _():
                for c in group:
                    c.copy.start()

    def wait_recv(links):
        for here, group in grouped(links, False):
            @pl.when(here)
            def _():
                for c in group:
                    c.copy.wait_recv()

    def wait_send(links):
        for here, group in grouped(links, True):
            @pl.when(here)
            def _():
                for c in group:
                    c.copy.wait_send()

    def x_from(d, w):
        return pl.ds(nx - w, w) if d > 0 else pl.ds(0, w)

    def x_to(d, w):
        return pl.ds(X0 - w, w) if d > 0 else pl.ds(X1, w)

    def y_from(d, w):
        return pl.ds(ny - w, w) if d > 0 else pl.ds(0, w)

    def y_to(d, w):
        return pl.ds(YE - w, w) if d > 0 else pl.ds(ny, w)

    def input_link(src, dst, side, wx, wy):
        dx, dy = side
        xs = (x_from(dx, wx), x_to(dx, wx)) if dx else (pl.ds(0, nx), own)
        ys = (y_from(dy, wy), y_to(dy, wy)) if dy else (rows, rows)
        return link(src.at[xs[0], ys[0]], dst.at[xs[1], ys[1]], side)

    def field_link(buf, side, wx, wy):
        dx, dy = side
        xs = (pl.ds(X1 - wx, wx) if dx > 0 else pl.ds(X0, wx), x_to(dx, wx)) if dx else (own, own)
        ys = (y_from(dy, wy), y_to(dy, wy)) if dy else (rows, rows)
        return link(buf.at[xs[0], ys[0]], buf.at[xs[1], ys[1]], side)

    def strips(planes):
        return [link(G.at[planes, y_from(d, w)], G.at[planes, y_to(d, w)], (0, d)) for d, w in ((1, 3), (-1, 4))]

    def heights_link(side):
        return link(h_in, HB.at[1 - side[0], 1 - side[1]], side)

    flat = [(-1, 0), (1, 0)]
    tall = [(0, -1), (0, 1)]
    hy = [heights_link(d) for d in tall]
    hx = [heights_link(d) for d in flat + diagonals]
    ty = [input_link(t_in, T, d, 0, 3) for d in tall] + [field_link(C, d, 0, 2) for d in tall]
    dy = [input_link(m_in, D, d, 0, 1) for d in tall]
    tx = [input_link(t_in, T, d, 2, 2) for d in diagonals]
    first, second = [], []
    if nbx == 4:
        tops, lows = (t_in.at[x_from(1, 3)], T.at[x_to(1, 3), rows]), (t_in.at[x_from(-1, 3)], T.at[x_to(-1, 3), rows])
        first = [link(tops[0], RB, (2, 0), (1, 3)), link(lows[0], RB, (-2, 0), (2, 0))]
        tx += [link(*tops, (1, 0), (0, 1)), link(*tops, (1, 0), (2, 3)), link(*lows, (-1, 0), (1, 0)), link(*lows, (-1, 0), (3, 2))]
        second = [link(RB, tops[1], (-1, 0), (3, 2)), link(RB, lows[1], (1, 0), (0, 1))]
    else:
        tx += [input_link(t_in, T, d, 3, 0) for d in flat]
    cx = [field_link(C, d, 2, 0) for d in flat] + [field_link(C, d, 1, 1) for d in diagonals]
    dx = [input_link(m_in, D, d, 1, 0) for d in flat]

    def zero_planes(lo):
        for buf in (T, D, G):
            buf[pl.ds(lo, X0)] = jnp.zeros((X0, YE, nz), jnp.float32)

    def zero_rows(lo):
        for buf in (T, D, G):
            buf[:, pl.ds(lo, 4), :] = jnp.zeros((XE, 4, nz), jnp.float32)

    pl.when(jnp.logical_not(has[-1]))(lambda: zero_planes(0))
    pl.when(jnp.logical_not(has[1]))(lambda: zero_planes(X1))
    pl.when(jnp.logical_not(hasy[1]))(lambda: zero_rows(ny))
    pl.when(jnp.logical_not(hasy[-1]))(lambda: zero_rows(ny + 4))

    def column(side, part, x, n, first):
        line = HB[side, part, pl.ds(x, 1), :].astype(jnp.float32)
        lanes = lax.broadcasted_iota(jnp.int32, (n, ny), 1)
        subs = lax.broadcasted_iota(jnp.int32, (n, ny), 0) + first
        return jnp.sum(jnp.where(lanes == subs, line, 0.0), axis=1, keepdims=True)

    def level_mask(col, high):
        level = lax.broadcasted_iota(jnp.int32, (col.shape[0], nz), 1).astype(jnp.float32)
        return jnp.where(level < col, high, 0.0)

    def obstacles(side, x, i):
        D4[i, rows, :] = level_mask(column(side, 1, x, ny, 0), ABSORB)

    def beyond_obstacles(side, x, i):
        col = jnp.where(lax.broadcasted_iota(jnp.int32, (8, 1), 0) < 4,
                        column(side, 2, x, 8, 0), column(side, 0, x, 8, ny - 8))
        D4[i, beyond, :] = level_mask(col, ABSORB)

    def cost(i, part):
        C[i, part, :] = POT[i - X0] + COUPLE * D[i, part, :] + (PENALTY / ABSORB) * D4[i, part, :]

    row8 = lax.broadcasted_iota(jnp.int32, (8, nz), 0)
    keep = (row8 >= jnp.where(hasy[1], 0, 4)) & (row8 < jnp.where(hasy[-1], 8, 4))

    def loop(lo, hi, f):
        step = 4 if (hi - lo) % 4 == 0 else 1

        @pl.loop(0, (hi - lo) // step)
        def _(j):
            for k in range(step):
                f(lo + step * j + k)

    def pairs(lo, hi, value, store):
        @pl.loop(0, (hi - lo) // 2)
        def _(j):
            i = lo + 2 * j
            a, b = value(i), value(i + 1)
            store(i, a)
            store(i + 1, b)

    def each(planes, value, store):
        for i in planes:
            store(i, value(i))

    def ends(k, e, value, store):
        @pl.loop(0, k + e)
        def _(j):
            i, n = X0 - k + j, X1 - e + j
            a, b = value(i), value(n)
            store(i, a)
            store(n, b)

    def clear(buf, low, high):
        def zero(lo, k):
            buf[pl.ds(lo, k)] = jnp.zeros((k, YE, nz), jnp.float32)
        if low:
            pl.when(jnp.logical_not(has[-1]))(lambda: zero(X0 - low, low))
        if high:
            pl.when(jnp.logical_not(has[1]))(lambda: zero(X1, high))

    lane = lax.broadcasted_iota(jnp.int32, (YE, 128), 1)

    def z_up(v):
        n = v.shape[0]
        tiles = [pltpu.roll(v[:, j:j + 128], 127, 1) for j in range(0, nz, 128)]
        tiles.append(jnp.zeros_like(tiles[0]))
        return jnp.concatenate([jnp.where(lane[:n] == 127, b, a) for a, b in zip(tiles, tiles[1:])], axis=1)

    def z_low(v, edge=None):
        n = v.shape[0]
        tiles = [jnp.zeros((n, 128), jnp.float32) if edge is None else edge]
        tiles += [pltpu.roll(v[:, j:j + 128], 1, 1) for j in range(0, nz, 128)]
        return jnp.concatenate([jnp.where(lane[:n] == 0, a, b) for a, b in zip(tiles, tiles[1:])], axis=1)

    def put(dst, i, v):
        dst[i, rows, :] = v[:ny]
        dst[i, beyond, :] = jnp.where(keep, v[ny:], 0.0)

    def hjb(src):
        def f(i):
            v = src[i]
            lap = -6.0 * v
            ham = jnp.zeros_like(v)
            for u, l in ((src[i + 1], src[i - 1]), (pltpu.roll(v, YE - 1, 0), pltpu.roll(v, 1, 0)),
                         (z_up(v), z_low(v))):
                lap = lap + (u + l)
                ham = ham + jnp.square(jnp.maximum(v - l, 0.0)) + jnp.square(jnp.minimum(u - v, 0.0))
            return v + DT_HJB * (NU_HJB * lap - 0.5 * ham + C[i])
        return f

    def put_mid(i, v):
        put(M, i, v)

    def put_halo(i, v):
        put(V, i, v)

    def put_value(i, v):
        put(V, i, v)
        v_out[i - X0] = v[:ny]

    def flux(v, vu, m, mu):
        s = v - vu
        return jnp.maximum(s, 0.0) * m + jnp.minimum(s, 0.0) * mu

    def x_flux(i):
        return flux(V[i, rows, :], V[i + 1, rows, :], D[i, rows, :], D[i + 1, rows, :])

    def transport(starts, n):
        def one(i, before):
            v, m = V[i], D[i]
            fy = flux(v, pltpu.roll(v, YE - 1, 0), m, pltpu.roll(m, YE - 1, 0))
            ly = pltpu.roll(fy, 1, 0)[:ny]
            v, m = v[:ny], m[:ny]
            fz = flux(v, z_up(v), m, z_up(m))
            lz = z_low(fz, jnp.minimum(-v[:, :128], 0.0) * m[:, :128])
            fx = x_flux(i)
            return fx, m - DT_FP * ((fx - before) + (fy[:ny] - ly) + (fz - lz))

        def f(j, before):
            done = [one(lo + j, b) for lo, b in zip(starts, before)]
            for lo, d in zip(starts, done):
                G[lo + j, rows, :] = d[1]
            return tuple(d[0] for d in done)
        lax.fori_loop(0, n, f, tuple(x_flux(lo - 1) for lo in starts))

    half = nx // 2
    for c in loads[:3]:
        c.wait()

    def own_cost(i):
        obstacles(1, i - X0, i)
        cost(i, rows)

    loop(X0, X1, own_cost)
    pl.semaphore_wait(barrier, greeted)
    start(first + ty + dy + tx + cx + dx + hx + hy)
    loads[3].wait()
    wait_recv(ty)
    wait_recv(first)
    start(second)
    pairs(X0 + 1, X1 - 1, hjb(T), put_mid)
    pairs(X0 + 2, X1 - 2, hjb(M), put_value)
    wait_recv(dy)
    transport((X0 + 3, X0 + half), half - 3)
    gi = strips(pl.ds(X0 + 3, nx - 6)) + [link(G.at[X0 + 3, rows], G.at[X1 + 3, rows], (-1, 0))]
    start(gi)

    wait_recv(hy)
    loop(X0, X1, lambda i: beyond_obstacles(1, i - X0, i))
    wait_recv(hx)

    def halo_obstacles(side, x, i):
        obstacles(side, x, i)
        beyond_obstacles(side, x, i)

    for j in range(2):
        halo_obstacles(0, nx - 2 + j, X0 - 2 + j)
    for j in range(3):
        halo_obstacles(2, j, X1 + j)

    wait_recv(tx + cx + second)
    ends(2, 1, hjb(T), put_mid)
    clear(M, 2, 2)
    ends(0, 2, hjb(M), put_value)
    for i in (X0 - 1, X1):
        put_halo(i, hjb(M)(i))
    clear(V, 1, 1)
    wait_recv(dx)
    transport((X0, X1 - 3), 3)

    gx = [field_link(G, d, 3, 0) for d in flat] + [field_link(G, d, 3, 3) for d in diagonals]
    gy = strips(pl.ds(X0, 3)) + strips(pl.ds(X1 - 3, 3))
    start(gy + gx)

    def shifted(src):
        def f(i):
            v = src[i]
            return D4[i] * v - ((src[i + 1] + src[i - 1]) + (pltpu.roll(v, YE - 1, 0) + pltpu.roll(v, 1, 0))
                                + (z_up(v) + z_low(v)))
        return f

    R = M

    def residual(i):
        return (1.0 - SHIFT) * G[i] - shifted(G)(i)

    def into(dst):
        return lambda i, v: put(dst, i, v)

    def moments(i, sums):
        r, b = R[i, rows, :], B1[i, rows, :]
        full = Q[i]
        yu = pltpu.roll(full, YE - 1, 0)[:ny]
        q = full[:ny]
        image = D4[i, rows, :] * q - 2.0 * (Q[i + 1, rows, :] + yu + z_up(q))
        terms = (r * r, r * b, b * b, b * q, q * q, q * image)

        def fold(a):
            a = a.reshape(ny // 8, 8, nz).sum(axis=0)
            return sum(a[:, j:j + 128] for j in range(0, nz, 128))

        return tuple(s + fold(a) for s, a in zip(sums, terms))

    wait_recv(gi[:2])
    pairs(X0 + 4, X1 - 4, residual, into(R))
    wait_recv(gy)
    ends(-1, 4, residual, into(R))
    pairs(X0 + 2, X1 - 2, shifted(R), into(B1))
    pairs(X0 + 3, X1 - 3, shifted(B1), into(Q))

    def two(j, sums):
        return moments(X0 + 4 + 2 * j, moments(X0 + 3 + 2 * j, sums))

    zero = jnp.zeros((8, 128), jnp.float32)
    sums = lax.fori_loop(0, (nx - 8) // 2, two, (zero,) * 6)

    wait_recv(gx + gi[2:])
    ends(2, 1, residual, into(R))
    into(R)(X1 + 2, residual(X1 + 2))
    clear(R, 2, 3)
    ends(1, 2, shifted(R), into(B1))
    into(B1)(X1 + 1, shifted(R)(X1 + 1))
    clear(B1, 1, 2)
    ends(0, 3, shifted(B1), into(Q))
    into(Q)(X1, shifted(B1)(X1))
    clear(Q, 0, 1)

    def rest(j, sums):
        for k in (2 * j, 2 * j + 1):
            sums = moments(X0 + k + jnp.where(k >= 3, nx - 8, 0), sums)
        return sums

    sums = lax.fori_loop(0, 4, rest, sums)
    tile_row = lax.broadcasted_iota(jnp.int32, (8, 128), 0)
    tile = zero
    for k, s in enumerate(sums):
        tile = jnp.where(tile_row == k, jnp.sum(s, axis=0, keepdims=True), tile)
    tile = jnp.sum(tile, axis=1, keepdims=True)
    tile = jnp.sum(jnp.where(tile_row == lane[:8], tile, 0.0), axis=0, keepdims=True)

    def all_sum(slots, value, n, me, device, send, recv):
        slots[me] = value
        copies = []
        for k in range(1, n):
            c = pltpu.make_async_remote_copy(
                src_ref=slots.at[me], dst_ref=slots.at[me], send_sem=send.at[k - 1], recv_sem=recv.at[k - 1],
                device_id=device(lax.rem(me + k, n)), device_id_type=MESH)
            c.start()
            copies.append(c)
        for k in range(1, n):
            source = lax.rem(me + n - k, n)
            pltpu.make_async_remote_copy(
                src_ref=slots.at[source], dst_ref=slots.at[source], send_sem=send.at[k - 1], recv_sem=recv.at[k - 1],
                device_id=device(source), device_id_type=MESH).wait_recv()
        return copies, jnp.sum(slots[...], axis=0)

    if whole:
        me = bx * nby + by
        PA[me] = tile
        ca, cb = [], []
        order = sorted(range(len(peers)), key=lambda k: -min(peers[k][1], nby - peers[k][1]))
        for k in order:
            c = pltpu.make_async_remote_copy(
                src_ref=PA.at[me], dst_ref=PA.at[me], send_sem=asend.at[k], recv_sem=arecv.at[k],
                device_id=peer(*peers[k]), device_id_type=MESH)
            c.start()
            ca.append(c)
        for k in order:
            x, y = peer(nbx - peers[k][0], nby - peers[k][1])
            source = x * nby + y
            pltpu.make_async_remote_copy(
                src_ref=PA.at[source], dst_ref=PA.at[source], send_sem=asend.at[k], recv_sem=arecv.at[k],
                device_id=(x, y), device_id_type=MESH).wait_recv()
        tile = jnp.sum(PA[...], axis=0)
    else:
        ca, tile = all_sum(PA, tile, nby, by, lambda j: (bx, j), asend, arecv)
        cb, tile = all_sum(PB, tile, nbx, bx, lambda j: (j, by), bsend, brecv)
    nu = [jnp.broadcast_to(tile[:, k:k + 1], (1, 128)) for k in range(6)]

    def dot(p, q, s):
        total = 0.0
        for i, a in enumerate(p):
            for j, b in enumerate(q):
                total = total + a * b * nu[i + j + s]
        return total

    def energy(p):
        return SHIFT * dot(p, p, 0) + dot(p, p, 1)

    def step_of(rr, p):
        return jnp.clip(rr / energy(p), 1.0 / 17.0, 1.0)

    one = jnp.ones_like(nu[0])
    rr = nu[0]
    p, r = (one,), (one,)
    x = None
    for it in range(3):
        a = step_of(rr, p)
        x = [a * c for c in p] if x is None else [x[j] + a * p[j] if j < len(x) else a * p[j] for j in range(len(p))]
        if it == 2:
            break
        image = [SHIFT * c for c in p] + [jnp.zeros_like(one)]
        for j, c in enumerate(p):
            image[j + 1] = image[j + 1] + c
        r = tuple((r[j] if j < len(r) else 0.0) - a * image[j] for j in range(len(image)))
        new = jnp.maximum(dot(r, r, 0), 0.0)
        beta = new / rr
        p = tuple(r[j] + (beta * p[j] if j < len(p) else 0.0) for j in range(len(r)))
        rr = new
    x = [jnp.concatenate([c] * (nz // 128), axis=1) for c in x]

    def finish(i):
        s_out[i - X0] = G[i, rows, :] + x[0] * R[i, rows, :] + x[1] * B1[i, rows, :] + x[2] * Q[i, rows, :]

    loop(X0, X1, finish)

    wait_send(first + second + hx + hy + ty + dy + tx + cx + dx + gi + gx + gy)
    for c in ca + cb:
        c.wait_send()


LINKS = 64


def write(v, s, v_out, s_out, sem):
    copies = [pltpu.make_async_copy(v, v_out, sem.at[0]), pltpu.make_async_copy(s, s_out, sem.at[1])]
    for c in copies:
        c.start()
    for c in copies:
        c.wait()


def per_device(nbx, nby, t, m, p, h):
    nx, ny, nz = t.shape
    slots = nbx * nby if nbx * nby <= ONE_STAGE else nby
    ext = pltpu.VMEM((nx + 2 * X0, ny + HALO, nz), jnp.float32)
    out = jax.ShapeDtypeStruct(t.shape, jnp.float32)
    v, s = pl.pallas_call(
        functools.partial(kernel, nbx, nby),
        out_shape=(out, out),
        in_specs=[pl.BlockSpec(memory_space=pl.ANY)] * 4,
        out_specs=(pl.BlockSpec(memory_space=pltpu.VMEM),) * 2,
        scratch_shapes=[ext] * 9 + [
            pltpu.VMEM((nx, ny, nz), jnp.float32),
            pltpu.VMEM((3, ny, nz), jnp.float32),
            pltpu.VMEM((3, 3, nx, ny), jnp.int32),
            pltpu.VMEM((slots, 1, 128), jnp.float32), pltpu.VMEM((nbx, 1, 128), jnp.float32),
            pltpu.SemaphoreType.DMA((LINKS,)), pltpu.SemaphoreType.DMA((LINKS,)),
            pltpu.SemaphoreType.DMA((slots - 1,)), pltpu.SemaphoreType.DMA((slots - 1,)),
            pltpu.SemaphoreType.DMA((nbx - 1,)), pltpu.SemaphoreType.DMA((nbx - 1,)),
            pltpu.SemaphoreType.DMA((4,)),
        ],
        compiler_params=pltpu.CompilerParams(collective_id=0, has_side_effects=True, vmem_limit_bytes=VMEM_LIMIT),
        name="mean_field_step",
    )(*(pltpu.with_memory_space_constraint(a, pltpu.HBM) for a in (t, m, p, h)))
    return pl.pallas_call(
        write,
        out_shape=(out, out),
        in_specs=[pl.BlockSpec(memory_space=pltpu.VMEM)] * 2,
        out_specs=(pl.BlockSpec(memory_space=pl.ANY),) * 2,
        scratch_shapes=[pltpu.SemaphoreType.DMA((2,))],
        compiler_params=pltpu.CompilerParams(vmem_limit_bytes=4_000_000),
        name="write",
    )(v, s)


def solution(mesh):
    cells, plane = P_("bx", "by", None), P_("bx", "by")
    return jax.shard_map(
        functools.partial(per_device, mesh.shape["bx"], mesh.shape["by"]),
        mesh=mesh, in_specs=(cells, cells, cells, plane), out_specs=(cells, cells), check_vma=False)
```

```python
import functools

import jax
import jax.numpy as jnp
from jax import lax
from jax.experimental import pallas as pl
from jax.experimental.pallas import tpu as pltpu
from jax.sharding import PartitionSpec as P_

DT_HJB = 0.5
NU_HJB = 0.25
COUPLE = 0.5
PENALTY = 2.0
DT_FP = 0.25
ABSORB = 4.0
SHIFT = 7.0

X0 = 4
HALO = 8
VMEM_LIMIT = 56_000_000
MESH = pl.DeviceIdType.MESH


class Link:
    def __init__(self, src, dst, send, recv, device, side, relay=None):
        self.copy = pltpu.make_async_remote_copy(
            src_ref=src, dst_ref=dst, send_sem=send, recv_sem=recv,
            device_id=device, device_id_type=MESH)
        self.side = side
        self.relay = relay


def kernel(nbx, nby, t_in, m_in, p_in, h_in, v_out, s_out,
           T, C, D, M, V, G, B1, Q, D4, POT, RB, HB, PA, PB,
           ssem, rsem, asend, arecv, bsend, brecv, lsem, token):
    nx, ny, nz = v_out.shape
    bx, by = lax.axis_index("bx"), lax.axis_index("by")
    XE, YE, X1 = nx + 2 * X0, ny + HALO, X0 + nx
    has = {-1: bx > 0, 1: bx < nbx - 1}
    hasy = {-1: by > 0, 1: by < nby - 1}

    def exists(dx, dy):
        if dx == 0:
            return hasy[dy]
        if dy == 0:
            return has[dx]
        return has[dx] & hasy[dy]

    sides = [(dx, dy) for dx in (-1, 0, 1) for dy in (-1, 0, 1) if (dx, dy) != (0, 0)]
    diagonals = [d for d in sides if d[0] and d[1]]
    there = {d: exists(*d) for d in sides}

    barrier = pltpu.get_barrier_semaphore()
    whole = nbx <= 4 and nby <= 8
    lines = [(0, j) for j in range(1, nby)] + [(i, 0) for i in range(1, nbx)]
    peers = [(i, j) for j in range(nby) for i in range(nbx) if (i, j) != (0, 0)] if whole else lines

    def peer(i, j):
        return lax.rem(bx + i, nbx), lax.rem(by + j, nby)

    greeted = 0
    if whole:
        greet = sides
        if nbx == 4:
            pl.semaphore_signal(barrier, inc=1, device_id=peer(2, 0), device_id_type=MESH)
            greeted = 1
    else:
        greet = diagonals
        for d in lines:
            pl.semaphore_signal(barrier, inc=1, device_id=peer(*d), device_id_type=MESH)
        greeted = len(lines)
    for d in greet:
        @pl.when(there[d])
        def _():
            pl.semaphore_signal(barrier, inc=1, device_id=(bx + d[0], by + d[1]), device_id_type=MESH)
        greeted = greeted + there[d].astype(jnp.int32)

    def far(k):
        return (by >= k, by - k), (by < nby - k, by + k)

    def tell(k, sem):
        for here, j in far(k):
            @pl.when(here)
            def _():
                pl.semaphore_signal(sem, inc=1, device_id=(bx, j), device_id_type=MESH)

    def hear(k, sem):
        pl.semaphore_wait(sem, sum(here.astype(jnp.int32) for here, _ in far(k)))

    rows = pl.ds(0, ny)
    beyond = pl.ds(ny, HALO)
    own = pl.ds(X0, nx)
    loads = [
        pltpu.make_async_copy(h_in, HB.at[1, 1], lsem.at[3]),
        pltpu.make_async_copy(m_in, D.at[own, rows], lsem.at[1]),
        pltpu.make_async_copy(p_in, POT, lsem.at[2]),
        pltpu.make_async_copy(t_in, T.at[own, rows], lsem.at[0]),
    ]
    for c in loads:
        c.start()

    count = [0]

    def link(src, dst, side, relay=None):
        i = count[0]
        count[0] += 1
        return Link(src, dst, ssem.at[i], rsem.at[i], (bx + side[0], by + side[1]), side, relay)

    def grouped(links, sends):
        groups = {}
        for c in links:
            groups.setdefault((c.side, c.relay), []).append(c)
        for (side, relay), group in groups.items():
            if relay is not None:
                here = bx == relay[0 if sends else 1]
            else:
                here = there[side] if sends else there[(-side[0], -side[1])]
            yield here, group

    def start(links):
        for here, group in grouped(links, True):
            @pl.when(here)
            def _():
                for c in group:
                    c.copy.start()

    def wait_recv(links):
        for here, group in grouped(links, False):
            @pl.when(here)
            def _():
                for c in group:
                    c.copy.wait_recv()

    def wait_send(links):
        for here, group in grouped(links, True):
            @pl.when(here)
            def _():
                for c in group:
                    c.copy.wait_send()

    def x_from(d, w):
        return pl.ds(nx - w, w) if d > 0 else pl.ds(0, w)

    def x_to(d, w):
        return pl.ds(X0 - w, w) if d > 0 else pl.ds(X1, w)

    def y_from(d, w):
        return pl.ds(ny - w, w) if d > 0 else pl.ds(0, w)

    def y_to(d, w):
        return pl.ds(YE - w, w) if d > 0 else pl.ds(ny, w)

    def input_link(src, dst, side, wx, wy):
        dx, dy = side
        xs = (x_from(dx, wx), x_to(dx, wx)) if dx else (pl.ds(0, nx), own)
        ys = (y_from(dy, wy), y_to(dy, wy)) if dy else (rows, rows)
        return link(src.at[xs[0], ys[0]], dst.at[xs[1], ys[1]], side)

    def field_link(buf, side, wx, wy):
        dx, dy = side
        xs = (pl.ds(X1 - wx, wx) if dx > 0 else pl.ds(X0, wx), x_to(dx, wx)) if dx else (own, own)
        ys = (y_from(dy, wy), y_to(dy, wy)) if dy else (rows, rows)
        return link(buf.at[xs[0], ys[0]], buf.at[xs[1], ys[1]], side)

    def strips(planes):
        return [link(G.at[planes, y_from(d, w)], G.at[planes, y_to(d, w)], (0, d)) for d, w in ((1, 3), (-1, 4))]

    def heights_link(side):
        return link(h_in, HB.at[1 - side[0], 1 - side[1]], side)

    flat = [(-1, 0), (1, 0)]
    tall = [(0, -1), (0, 1)]
    hy = [heights_link(d) for d in tall]
    hx = [heights_link(d) for d in flat + diagonals]
    ty = [input_link(t_in, T, d, 0, 3) for d in tall]
    cy = [field_link(C, d, 0, 2) for d in tall]
    dy = [input_link(m_in, D, d, 0, 1) for d in tall]
    tx = [input_link(t_in, T, d, 2, 2) for d in diagonals]
    first, second = [], []
    if nbx == 4:
        tops, lows = (t_in.at[x_from(1, 3)], T.at[x_to(1, 3), rows]), (t_in.at[x_from(-1, 3)], T.at[x_to(-1, 3), rows])
        first = [link(tops[0], RB, (2, 0), (1, 3)), link(lows[0], RB, (-2, 0), (2, 0))]
        tx += [link(*tops, (1, 0), (0, 1)), link(*tops, (1, 0), (2, 3)), link(*lows, (-1, 0), (1, 0)), link(*lows, (-1, 0), (3, 2))]
        second = [link(RB, tops[1], (-1, 0), (3, 2)), link(RB, lows[1], (1, 0), (0, 1))]
    else:
        tx += [input_link(t_in, T, d, 3, 0) for d in flat]
    cx = [field_link(C, d, 2, 0) for d in flat] + [field_link(C, d, 1, 1) for d in diagonals]
    dx = [input_link(m_in, D, d, 1, 0) for d in flat]

    def zero_planes(lo):
        for buf in (T, D, G):
            buf[pl.ds(lo, X0)] = jnp.zeros((X0, YE, nz), jnp.float32)

    def zero_rows(lo):
        for buf in (T, D, G):
            buf[:, pl.ds(lo, 4), :] = jnp.zeros((XE, 4, nz), jnp.float32)

    pl.when(jnp.logical_not(has[-1]))(lambda: zero_planes(0))
    pl.when(jnp.logical_not(has[1]))(lambda: zero_planes(X1))
    pl.when(jnp.logical_not(hasy[1]))(lambda: zero_rows(ny))
    pl.when(jnp.logical_not(hasy[-1]))(lambda: zero_rows(ny + 4))

    def column(side, part, x, n, first):
        line = HB[side, part, pl.ds(x, 1), :].astype(jnp.float32)
        lanes = lax.broadcasted_iota(jnp.int32, (n, ny), 1)
        subs = lax.broadcasted_iota(jnp.int32, (n, ny), 0) + first
        return jnp.sum(jnp.where(lanes == subs, line, 0.0), axis=1, keepdims=True)

    def level_mask(col, high):
        level = lax.broadcasted_iota(jnp.int32, (col.shape[0], nz), 1).astype(jnp.float32)
        return jnp.where(level < col, high, 0.0)

    def obstacles(side, x, i):
        D4[i, rows, :] = level_mask(column(side, 1, x, ny, 0), ABSORB)

    def beyond_obstacles(side, x, i):
        col = jnp.where(lax.broadcasted_iota(jnp.int32, (8, 1), 0) < 4,
                        column(side, 2, x, 8, 0), column(side, 0, x, 8, ny - 8))
        D4[i, beyond, :] = level_mask(col, ABSORB)

    def cost(i, part):
        C[i, part, :] = POT[i - X0] + COUPLE * D[i, part, :] + (PENALTY / ABSORB) * D4[i, part, :]

    row8 = lax.broadcasted_iota(jnp.int32, (8, nz), 0)
    keep = (row8 >= jnp.where(hasy[1], 0, 4)) & (row8 < jnp.where(hasy[-1], 8, 4))

    def loop(lo, hi, f):
        step = 4 if (hi - lo) % 4 == 0 else 1

        @pl.loop(0, (hi - lo) // step)
        def _(j):
            for k in range(step):
                f(lo + step * j + k)

    def pairs(lo, hi, value, store):
        @pl.loop(0, (hi - lo) // 2)
        def _(j):
            i = lo + 2 * j
            a, b = value(i), value(i + 1)
            store(i, a)
            store(i + 1, b)

    def each(planes, value, store):
        for i in planes:
            store(i, value(i))

    def ends(k, e, value, store):
        @pl.loop(0, k + e)
        def _(j):
            i, n = X0 - k + j, X1 - e + j
            a, b = value(i), value(n)
            store(i, a)
            store(n, b)

    def clear(buf, low, high):
        def zero(lo, k):
            buf[pl.ds(lo, k)] = jnp.zeros((k, YE, nz), jnp.float32)
        if low:
            pl.when(jnp.logical_not(has[-1]))(lambda: zero(X0 - low, low))
        if high:
            pl.when(jnp.logical_not(has[1]))(lambda: zero(X1, high))

    lane = lax.broadcasted_iota(jnp.int32, (YE, 128), 1)

    def z_up(v):
        n = v.shape[0]
        tiles = [pltpu.roll(v[:, j:j + 128], 127, 1) for j in range(0, nz, 128)]
        tiles.append(jnp.zeros_like(tiles[0]))
        return jnp.concatenate([jnp.where(lane[:n] == 127, b, a) for a, b in zip(tiles, tiles[1:])], axis=1)

    def z_low(v, edge=None):
        n = v.shape[0]
        tiles = [jnp.zeros((n, 128), jnp.float32) if edge is None else edge]
        tiles += [pltpu.roll(v[:, j:j + 128], 1, 1) for j in range(0, nz, 128)]
        return jnp.concatenate([jnp.where(lane[:n] == 0, a, b) for a, b in zip(tiles, tiles[1:])], axis=1)

    def put(dst, i, v):
        dst[i, rows, :] = v[:ny]
        dst[i, beyond, :] = jnp.where(keep, v[ny:], 0.0)

    def hjb(src):
        def f(i):
            v = src[i]
            lap = -6.0 * v
            ham = jnp.zeros_like(v)
            for u, l in ((src[i + 1], src[i - 1]), (pltpu.roll(v, YE - 1, 0), pltpu.roll(v, 1, 0)),
                         (z_up(v), z_low(v))):
                lap = lap + (u + l)
                ham = ham + jnp.square(jnp.maximum(v - l, 0.0)) + jnp.square(jnp.minimum(u - v, 0.0))
            return v + DT_HJB * (NU_HJB * lap - 0.5 * ham + C[i])
        return f

    def put_mid(i, v):
        put(M, i, v)

    def put_halo(i, v):
        put(V, i, v)

    def put_value(i, v):
        put(V, i, v)
        v_out[i - X0] = v[:ny]

    def flux(v, vu, m, mu):
        s = v - vu
        return jnp.maximum(s, 0.0) * m + jnp.minimum(s, 0.0) * mu

    def x_flux(i):
        return flux(V[i, rows, :], V[i + 1, rows, :], D[i, rows, :], D[i + 1, rows, :])

    def transport(starts, n):
        def one(i, before):
            v, m = V[i], D[i]
            fy = flux(v, pltpu.roll(v, YE - 1, 0), m, pltpu.roll(m, YE - 1, 0))
            ly = pltpu.roll(fy, 1, 0)[:ny]
            v, m = v[:ny], m[:ny]
            fz = flux(v, z_up(v), m, z_up(m))
            lz = z_low(fz, jnp.minimum(-v[:, :128], 0.0) * m[:, :128])
            fx = x_flux(i)
            return fx, m - DT_FP * ((fx - before) + (fy[:ny] - ly) + (fz - lz))

        def f(j, before):
            done = [one(lo + j, b) for lo, b in zip(starts, before)]
            for lo, d in zip(starts, done):
                G[lo + j, rows, :] = d[1]
            return tuple(d[0] for d in done)
        lax.fori_loop(0, n, f, tuple(x_flux(lo - 1) for lo in starts))

    half = nx // 2
    pl.semaphore_wait(barrier, greeted)
    start(first + ty + tx)
    for c in loads[:3]:
        c.wait()

    def own_cost(i):
        obstacles(1, i - X0, i)
        cost(i, rows)

    loop(X0, X1, own_cost)
    start(cy + cx + dy + dx + hx + hy)
    loads[3].wait()
    wait_recv(ty + cy)
    wait_recv(first)
    start(second)
    pairs(X0 + 1, X1 - 1, hjb(T), put_mid)
    pairs(X0 + 2, X1 - 2, hjb(M), put_value)
    wait_recv(dy)
    transport((X0 + 3, X0 + half), half - 3)
    gi = strips(pl.ds(X0 + 3, nx - 6)) + [link(G.at[X0 + 3, rows], G.at[X1 + 3, rows], (-1, 0))]
    start(gi)

    wait_recv(hy)
    loop(X0, X1, lambda i: beyond_obstacles(1, i - X0, i))
    wait_recv(hx)

    def halo_obstacles(side, x, i):
        obstacles(side, x, i)
        beyond_obstacles(side, x, i)

    for j in range(2):
        halo_obstacles(0, nx - 2 + j, X0 - 2 + j)
    for j in range(3):
        halo_obstacles(2, j, X1 + j)

    wait_recv(tx + cx + second)
    ends(2, 1, hjb(T), put_mid)
    clear(M, 2, 2)
    ends(0, 2, hjb(M), put_value)
    for i in (X0 - 1, X1):
        put_halo(i, hjb(M)(i))
    clear(V, 1, 1)
    wait_recv(dx)
    transport((X0, X1 - 3), 3)

    gx = [field_link(G, d, 3, 0) for d in flat] + [field_link(G, d, 3, 3) for d in diagonals]
    gy = strips(pl.ds(X0, 3)) + strips(pl.ds(X1 - 3, 3))
    start(gy + gx)
    if whole:
        tell(2, token.at[0])

    def shifted(src):
        def f(i):
            v = src[i]
            return D4[i] * v - ((src[i + 1] + src[i - 1]) + (pltpu.roll(v, YE - 1, 0) + pltpu.roll(v, 1, 0))
                                + (z_up(v) + z_low(v)))
        return f

    R = M

    def residual(i):
        return (1.0 - SHIFT) * G[i] - shifted(G)(i)

    def into(dst):
        return lambda i, v: put(dst, i, v)

    def moments(i, sums):
        r, b = R[i, rows, :], B1[i, rows, :]
        full = Q[i]
        yu = pltpu.roll(full, YE - 1, 0)[:ny]
        q = full[:ny]
        image = D4[i, rows, :] * q - 2.0 * (Q[i + 1, rows, :] + yu + z_up(q))
        terms = (r * r, r * b, b * b, b * q, q * q, q * image)

        def fold(a):
            a = a.reshape(ny // 8, 8, nz).sum(axis=0)
            return sum(a[:, j:j + 128] for j in range(0, nz, 128))

        return tuple(s + fold(a) for s, a in zip(sums, terms))

    wait_recv(gi[:2])
    pairs(X0 + 4, X1 - 4, residual, into(R))
    wait_recv(gy)
    ends(-1, 4, residual, into(R))
    pairs(X0 + 2, X1 - 2, shifted(R), into(B1))
    pairs(X0 + 3, X1 - 3, shifted(B1), into(Q))

    def two(j, sums):
        return moments(X0 + 4 + 2 * j, moments(X0 + 3 + 2 * j, sums))

    zero = jnp.zeros((8, 128), jnp.float32)
    sums = lax.fori_loop(0, (nx - 8) // 2, two, (zero,) * 6)

    wait_recv(gx + gi[2:])
    if whole:
        hear(2, token.at[0])
        tell(4, token.at[1])
    ends(2, 1, residual, into(R))
    into(R)(X1 + 2, residual(X1 + 2))
    clear(R, 2, 3)
    ends(1, 2, shifted(R), into(B1))
    into(B1)(X1 + 1, shifted(R)(X1 + 1))
    clear(B1, 1, 2)
    ends(0, 3, shifted(B1), into(Q))
    into(Q)(X1, shifted(B1)(X1))
    clear(Q, 0, 1)

    def rest(j, sums):
        for k in (2 * j, 2 * j + 1):
            sums = moments(X0 + k + jnp.where(k >= 3, nx - 8, 0), sums)
        return sums

    sums = lax.fori_loop(0, 4, rest, sums)
    tile_row = lax.broadcasted_iota(jnp.int32, (8, 128), 0)
    tile = zero
    for k, s in enumerate(sums):
        tile = jnp.where(tile_row == k, jnp.sum(s, axis=0, keepdims=True), tile)
    tile = jnp.sum(tile, axis=1, keepdims=True)
    tile = jnp.sum(jnp.where(tile_row == lane[:8], tile, 0.0), axis=0, keepdims=True)

    def all_sum(slots, value, n, me, device, send, recv):
        slots[me] = value
        copies = []
        for k in range(1, n):
            c = pltpu.make_async_remote_copy(
                src_ref=slots.at[me], dst_ref=slots.at[me], send_sem=send.at[k - 1], recv_sem=recv.at[k - 1],
                device_id=device(lax.rem(me + k, n)), device_id_type=MESH)
            c.start()
            copies.append(c)
        for k in range(1, n):
            source = lax.rem(me + n - k, n)
            pltpu.make_async_remote_copy(
                src_ref=slots.at[source], dst_ref=slots.at[source], send_sem=send.at[k - 1], recv_sem=recv.at[k - 1],
                device_id=device(source), device_id_type=MESH).wait_recv()
        return copies, jnp.sum(slots[...], axis=0)

    if whole:
        hear(4, token.at[1])
        me = bx * nby + by
        PA[me] = tile
        ca, cb = [], []
        order = sorted(range(len(peers)), key=lambda k: -min(peers[k][1], nby - peers[k][1]))
        for k in order:
            c = pltpu.make_async_remote_copy(
                src_ref=PA.at[me], dst_ref=PA.at[me], send_sem=asend.at[k], recv_sem=arecv.at[k],
                device_id=peer(*peers[k]), device_id_type=MESH)
            c.start()
            ca.append(c)
        for k in order:
            x, y = peer(nbx - peers[k][0], nby - peers[k][1])
            source = x * nby + y
            pltpu.make_async_remote_copy(
                src_ref=PA.at[source], dst_ref=PA.at[source], send_sem=asend.at[k], recv_sem=arecv.at[k],
                device_id=(x, y), device_id_type=MESH).wait_recv()
        tile = jnp.sum(PA[...], axis=0)
    else:
        ca, tile = all_sum(PA, tile, nby, by, lambda j: (bx, j), asend, arecv)
        cb, tile = all_sum(PB, tile, nbx, bx, lambda j: (j, by), bsend, brecv)
    nu = [jnp.broadcast_to(tile[:, k:k + 1], (1, 128)) for k in range(6)]

    def dot(p, q, s):
        total = 0.0
        for i, a in enumerate(p):
            for j, b in enumerate(q):
                total = total + a * b * nu[i + j + s]
        return total

    def energy(p):
        return SHIFT * dot(p, p, 0) + dot(p, p, 1)

    def step_of(rr, p):
        return jnp.clip(rr / energy(p), 1.0 / 17.0, 1.0)

    one = jnp.ones_like(nu[0])
    rr = nu[0]
    p, r = (one,), (one,)
    x = None
    for it in range(3):
        a = step_of(rr, p)
        x = [a * c for c in p] if x is None else [x[j] + a * p[j] if j < len(x) else a * p[j] for j in range(len(p))]
        if it == 2:
            break
        image = [SHIFT * c for c in p] + [jnp.zeros_like(one)]
        for j, c in enumerate(p):
            image[j + 1] = image[j + 1] + c
        r = tuple((r[j] if j < len(r) else 0.0) - a * image[j] for j in range(len(image)))
        new = jnp.maximum(dot(r, r, 0), 0.0)
        beta = new / rr
        p = tuple(r[j] + (beta * p[j] if j < len(p) else 0.0) for j in range(len(r)))
        rr = new
    x = [jnp.concatenate([c] * (nz // 128), axis=1) for c in x]

    def finish(i):
        s_out[i - X0] = G[i, rows, :] + x[0] * R[i, rows, :] + x[1] * B1[i, rows, :] + x[2] * Q[i, rows, :]

    loop(X0, X1, finish)

    wait_send(first + second + hx + hy + ty + cy + dy + tx + cx + dx + gi + gx + gy)
    for c in ca + cb:
        c.wait_send()


LINKS = 64


def write(v, s, v_out, s_out, sem):
    copies = [pltpu.make_async_copy(v, v_out, sem.at[0]), pltpu.make_async_copy(s, s_out, sem.at[1])]
    for c in copies:
        c.start()
    for c in copies:
        c.wait()


def per_device(nbx, nby, t, m, p, h):
    nx, ny, nz = t.shape
    slots = nbx * nby if nbx <= 4 and nby <= 8 else nby
    ext = pltpu.VMEM((nx + 2 * X0, ny + HALO, nz), jnp.float32)
    out = jax.ShapeDtypeStruct(t.shape, jnp.float32)
    v, s = pl.pallas_call(
        functools.partial(kernel, nbx, nby),
        out_shape=(out, out),
        in_specs=[pl.BlockSpec(memory_space=pl.ANY)] * 4,
        out_specs=(pl.BlockSpec(memory_space=pltpu.VMEM),) * 2,
        scratch_shapes=[ext] * 9 + [
            pltpu.VMEM((nx, ny, nz), jnp.float32),
            pltpu.VMEM((3, ny, nz), jnp.float32),
            pltpu.VMEM((3, 3, nx, ny), jnp.int32),
            pltpu.VMEM((slots, 1, 128), jnp.float32), pltpu.VMEM((nbx, 1, 128), jnp.float32),
            pltpu.SemaphoreType.DMA((LINKS,)), pltpu.SemaphoreType.DMA((LINKS,)),
            pltpu.SemaphoreType.DMA((slots - 1,)), pltpu.SemaphoreType.DMA((slots - 1,)),
            pltpu.SemaphoreType.DMA((nbx - 1,)), pltpu.SemaphoreType.DMA((nbx - 1,)),
            pltpu.SemaphoreType.DMA((4,)), pltpu.SemaphoreType.REGULAR((2,)),
        ],
        compiler_params=pltpu.CompilerParams(collective_id=0, has_side_effects=True, vmem_limit_bytes=VMEM_LIMIT),
        name="mean_field_step",
    )(*(pltpu.with_memory_space_constraint(a, pltpu.HBM) for a in (t, m, p, h)))
    return pl.pallas_call(
        write,
        out_shape=(out, out),
        in_specs=[pl.BlockSpec(memory_space=pltpu.VMEM)] * 2,
        out_specs=(pl.BlockSpec(memory_space=pl.ANY),) * 2,
        scratch_shapes=[pltpu.SemaphoreType.DMA((2,))],
        compiler_params=pltpu.CompilerParams(vmem_limit_bytes=4_000_000),
        name="write",
    )(v, s)


def solution(mesh):
    cells, plane = P_("bx", "by", None), P_("bx", "by")
    return jax.shard_map(
        functools.partial(per_device, mesh.shape["bx"], mesh.shape["by"]),
        mesh=mesh, in_specs=(cells, cells, cells, plane), out_specs=(cells, cells), check_vma=False)
```

```python
import functools

import jax
import jax.numpy as jnp
from jax import lax
from jax.experimental import pallas as pl
from jax.experimental.pallas import tpu as pltpu
from jax.sharding import PartitionSpec as P_

DT_HJB = 0.5
NU_HJB = 0.25
COUPLE = 0.5
PENALTY = 2.0
DT_FP = 0.25
ABSORB = 4.0
SHIFT = 7.0

X0 = 4
HALO = 8
VMEM_LIMIT = 56_000_000
MESH = pl.DeviceIdType.MESH


class Link:
    def __init__(self, src, dst, send, recv, device, side, relay=None):
        self.copy = pltpu.make_async_remote_copy(
            src_ref=src, dst_ref=dst, send_sem=send, recv_sem=recv,
            device_id=device, device_id_type=MESH)
        self.side = side
        self.relay = relay


def kernel(nbx, nby, t_in, m_in, p_in, h_in, v_out, s_out,
           T, C, D, M, V, G, B1, Q, D4, POT, RB, HB, PA, PB,
           ssem, rsem, asend, arecv, bsend, brecv, lsem, token):
    nx, ny, nz = v_out.shape
    bx, by = lax.axis_index("bx"), lax.axis_index("by")
    XE, YE, X1 = nx + 2 * X0, ny + HALO, X0 + nx
    has = {-1: bx > 0, 1: bx < nbx - 1}
    hasy = {-1: by > 0, 1: by < nby - 1}

    def exists(dx, dy):
        if dx == 0:
            return hasy[dy]
        if dy == 0:
            return has[dx]
        return has[dx] & hasy[dy]

    sides = [(dx, dy) for dx in (-1, 0, 1) for dy in (-1, 0, 1) if (dx, dy) != (0, 0)]
    diagonals = [d for d in sides if d[0] and d[1]]
    there = {d: exists(*d) for d in sides}

    barrier = pltpu.get_barrier_semaphore()
    whole = nbx <= 4 and nby <= 8
    lines = [(0, j) for j in range(1, nby)] + [(i, 0) for i in range(1, nbx)]
    peers = [(i, j) for j in range(nby) for i in range(nbx) if (i, j) != (0, 0)] if whole else lines

    def peer(i, j):
        return lax.rem(bx + i, nbx), lax.rem(by + j, nby)

    greeted = 0
    if whole:
        greet = sides
        if nbx == 4:
            pl.semaphore_signal(barrier, inc=1, device_id=peer(2, 0), device_id_type=MESH)
            greeted = 1
    else:
        greet = diagonals
        for d in lines:
            pl.semaphore_signal(barrier, inc=1, device_id=peer(*d), device_id_type=MESH)
        greeted = len(lines)
    for d in greet:
        @pl.when(there[d])
        def _():
            pl.semaphore_signal(barrier, inc=1, device_id=(bx + d[0], by + d[1]), device_id_type=MESH)
        greeted = greeted + there[d].astype(jnp.int32)

    def far(k):
        return (by >= k, by - k), (by < nby - k, by + k)

    def tell(k, sem):
        for here, j in far(k):
            @pl.when(here)
            def _():
                pl.semaphore_signal(sem, inc=1, device_id=(bx, j), device_id_type=MESH)

    def hear(k, sem):
        pl.semaphore_wait(sem, sum(here.astype(jnp.int32) for here, _ in far(k)))

    rows = pl.ds(0, ny)
    beyond = pl.ds(ny, HALO)
    own = pl.ds(X0, nx)
    loads = [
        pltpu.make_async_copy(h_in, HB.at[1, 1], lsem.at[3]),
        pltpu.make_async_copy(m_in, D.at[own, rows], lsem.at[1]),
        pltpu.make_async_copy(p_in, POT, lsem.at[2]),
        pltpu.make_async_copy(t_in, T.at[own, rows], lsem.at[0]),
    ]
    for c in loads:
        c.start()

    count = [0]

    def link(src, dst, side, relay=None):
        i = count[0]
        count[0] += 1
        return Link(src, dst, ssem.at[i], rsem.at[i], (bx + side[0], by + side[1]), side, relay)

    def grouped(links, sends):
        groups = {}
        for c in links:
            groups.setdefault((c.side, c.relay), []).append(c)
        for (side, relay), group in groups.items():
            if relay is not None:
                here = bx == relay[0 if sends else 1]
            else:
                here = there[side] if sends else there[(-side[0], -side[1])]
            yield here, group

    def start(links):
        for here, group in grouped(links, True):
            @pl.when(here)
            def _():
                for c in group:
                    c.copy.start()

    def wait_recv(links):
        for here, group in grouped(links, False):
            @pl.when(here)
            def _():
                for c in group:
                    c.copy.wait_recv()

    def wait_send(links):
        for here, group in grouped(links, True):
            @pl.when(here)
            def _():
                for c in group:
                    c.copy.wait_send()

    def x_from(d, w):
        return pl.ds(nx - w, w) if d > 0 else pl.ds(0, w)

    def x_to(d, w):
        return pl.ds(X0 - w, w) if d > 0 else pl.ds(X1, w)

    def y_from(d, w):
        return pl.ds(ny - w, w) if d > 0 else pl.ds(0, w)

    def y_to(d, w):
        return pl.ds(YE - w, w) if d > 0 else pl.ds(ny, w)

    def input_link(src, dst, side, wx, wy):
        dx, dy = side
        xs = (x_from(dx, wx), x_to(dx, wx)) if dx else (pl.ds(0, nx), own)
        ys = (y_from(dy, wy), y_to(dy, wy)) if dy else (rows, rows)
        return link(src.at[xs[0], ys[0]], dst.at[xs[1], ys[1]], side)

    def field_link(buf, side, wx, wy):
        dx, dy = side
        xs = (pl.ds(X1 - wx, wx) if dx > 0 else pl.ds(X0, wx), x_to(dx, wx)) if dx else (own, own)
        ys = (y_from(dy, wy), y_to(dy, wy)) if dy else (rows, rows)
        return link(buf.at[xs[0], ys[0]], buf.at[xs[1], ys[1]], side)

    def strips(planes):
        return [link(G.at[planes, y_from(d, w)], G.at[planes, y_to(d, w)], (0, d)) for d, w in ((1, 3), (-1, 4))]

    def heights_link(side):
        return link(h_in, HB.at[1 - side[0], 1 - side[1]], side)

    flat = [(-1, 0), (1, 0)]
    tall = [(0, -1), (0, 1)]
    hy = [heights_link(d) for d in tall]
    hx = [heights_link(d) for d in flat + diagonals]
    ty = [input_link(t_in, T, d, 0, 3) for d in tall]
    cy = [field_link(C, d, 0, 2) for d in tall]
    dy = [input_link(m_in, D, d, 0, 1) for d in tall]
    tx = [input_link(t_in, T, d, 2, 2) for d in diagonals]
    first, second = [], []
    if nbx == 4:
        tops, lows = (t_in.at[x_from(1, 3)], T.at[x_to(1, 3), rows]), (t_in.at[x_from(-1, 3)], T.at[x_to(-1, 3), rows])
        first = [link(tops[0], RB, (2, 0), (1, 3)), link(lows[0], RB, (-2, 0), (2, 0))]
        tx += [link(*tops, (1, 0), (0, 1)), link(*tops, (1, 0), (2, 3)), link(*lows, (-1, 0), (1, 0)), link(*lows, (-1, 0), (3, 2))]
        second = [link(RB, tops[1], (-1, 0), (3, 2)), link(RB, lows[1], (1, 0), (0, 1))]
    else:
        tx += [input_link(t_in, T, d, 3, 0) for d in flat]
    cx = [field_link(C, d, 2, 0) for d in flat] + [field_link(C, d, 1, 1) for d in diagonals]
    dx = [input_link(m_in, D, d, 1, 0) for d in flat]

    def zero_planes(lo):
        for buf in (T, D, G):
            buf[pl.ds(lo, X0)] = jnp.zeros((X0, YE, nz), jnp.float32)

    def zero_rows(lo):
        for buf in (T, D, G):
            buf[:, pl.ds(lo, 4), :] = jnp.zeros((XE, 4, nz), jnp.float32)

    pl.when(jnp.logical_not(has[-1]))(lambda: zero_planes(0))
    pl.when(jnp.logical_not(has[1]))(lambda: zero_planes(X1))
    pl.when(jnp.logical_not(hasy[1]))(lambda: zero_rows(ny))
    pl.when(jnp.logical_not(hasy[-1]))(lambda: zero_rows(ny + 4))

    def column(side, part, x, n, first):
        line = HB[side, part, pl.ds(x, 1), :].astype(jnp.float32)
        lanes = lax.broadcasted_iota(jnp.int32, (n, ny), 1)
        subs = lax.broadcasted_iota(jnp.int32, (n, ny), 0) + first
        return jnp.sum(jnp.where(lanes == subs, line, 0.0), axis=1, keepdims=True)

    def level_mask(col, high):
        level = lax.broadcasted_iota(jnp.int32, (col.shape[0], nz), 1).astype(jnp.float32)
        return jnp.where(level < col, high, 0.0)

    def obstacles(side, x, i):
        D4[i, rows, :] = level_mask(column(side, 1, x, ny, 0), ABSORB)

    def beyond_obstacles(side, x, i):
        col = jnp.where(lax.broadcasted_iota(jnp.int32, (8, 1), 0) < 4,
                        column(side, 2, x, 8, 0), column(side, 0, x, 8, ny - 8))
        D4[i, beyond, :] = level_mask(col, ABSORB)

    def cost(i, part):
        C[i, part, :] = POT[i - X0] + COUPLE * D[i, part, :] + (PENALTY / ABSORB) * D4[i, part, :]

    row8 = lax.broadcasted_iota(jnp.int32, (8, nz), 0)
    keep = (row8 >= jnp.where(hasy[1], 0, 4)) & (row8 < jnp.where(hasy[-1], 8, 4))

    def loop(lo, hi, f):
        step = 4 if (hi - lo) % 4 == 0 else 1

        @pl.loop(0, (hi - lo) // step)
        def _(j):
            for k in range(step):
                f(lo + step * j + k)

    def pairs(lo, hi, value, store):
        @pl.loop(0, (hi - lo) // 2)
        def _(j):
            i = lo + 2 * j
            a, b = value(i), value(i + 1)
            store(i, a)
            store(i + 1, b)

    def each(planes, value, store):
        for i in planes:
            store(i, value(i))

    def ends(k, e, value, store):
        @pl.loop(0, k + e)
        def _(j):
            i, n = X0 - k + j, X1 - e + j
            a, b = value(i), value(n)
            store(i, a)
            store(n, b)

    def clear(buf, low, high):
        def zero(lo, k):
            buf[pl.ds(lo, k)] = jnp.zeros((k, YE, nz), jnp.float32)
        if low:
            pl.when(jnp.logical_not(has[-1]))(lambda: zero(X0 - low, low))
        if high:
            pl.when(jnp.logical_not(has[1]))(lambda: zero(X1, high))

    lane = lax.broadcasted_iota(jnp.int32, (YE, 128), 1)

    def z_up(v):
        n = v.shape[0]
        tiles = [pltpu.roll(v[:, j:j + 128], 127, 1) for j in range(0, nz, 128)]
        tiles.append(jnp.zeros_like(tiles[0]))
        return jnp.concatenate([jnp.where(lane[:n] == 127, b, a) for a, b in zip(tiles, tiles[1:])], axis=1)

    def z_low(v, edge=None):
        n = v.shape[0]
        tiles = [jnp.zeros((n, 128), jnp.float32) if edge is None else edge]
        tiles += [pltpu.roll(v[:, j:j + 128], 1, 1) for j in range(0, nz, 128)]
        return jnp.concatenate([jnp.where(lane[:n] == 0, a, b) for a, b in zip(tiles, tiles[1:])], axis=1)

    def put(dst, i, v):
        dst[i, rows, :] = v[:ny]
        dst[i, beyond, :] = jnp.where(keep, v[ny:], 0.0)

    def hjb(src):
        def f(i):
            v = src[i]
            lap = -6.0 * v
            ham = jnp.zeros_like(v)
            for u, l in ((src[i + 1], src[i - 1]), (pltpu.roll(v, YE - 1, 0), pltpu.roll(v, 1, 0)),
                         (z_up(v), z_low(v))):
                lap = lap + (u + l)
                ham = ham + jnp.square(jnp.maximum(v - l, 0.0)) + jnp.square(jnp.minimum(u - v, 0.0))
            return v + DT_HJB * (NU_HJB * lap - 0.5 * ham + C[i])
        return f

    def put_mid(i, v):
        put(M, i, v)

    def put_halo(i, v):
        put(V, i, v)

    def put_value(i, v):
        put(V, i, v)
        v_out[i - X0] = v[:ny]

    def flux(v, vu, m, mu):
        s = v - vu
        return jnp.maximum(s, 0.0) * m + jnp.minimum(s, 0.0) * mu

    def x_flux(i):
        return flux(V[i, rows, :], V[i + 1, rows, :], D[i, rows, :], D[i + 1, rows, :])

    def transport(starts, n):
        def one(i, before):
            v, m = V[i], D[i]
            fy = flux(v, pltpu.roll(v, YE - 1, 0), m, pltpu.roll(m, YE - 1, 0))
            ly = pltpu.roll(fy, 1, 0)[:ny]
            v, m = v[:ny], m[:ny]
            fz = flux(v, z_up(v), m, z_up(m))
            lz = z_low(fz, jnp.minimum(-v[:, :128], 0.0) * m[:, :128])
            fx = x_flux(i)
            return fx, m - DT_FP * ((fx - before) + (fy[:ny] - ly) + (fz - lz))

        def f(j, before):
            done = [one(lo + j, b) for lo, b in zip(starts, before)]
            for lo, d in zip(starts, done):
                G[lo + j, rows, :] = d[1]
            return tuple(d[0] for d in done)
        lax.fori_loop(0, n, f, tuple(x_flux(lo - 1) for lo in starts))

    half = nx // 2
    pl.semaphore_wait(barrier, greeted)
    start(first + ty + tx)
    for c in loads[:3]:
        c.wait()

    def own_cost(i):
        obstacles(1, i - X0, i)
        cost(i, rows)

    loop(X0, X1, own_cost)
    start(cy + cx + dy + dx + hx + hy)
    loads[3].wait()
    wait_recv(ty + cy)
    wait_recv(first)
    start(second)
    pairs(X0 + 1, X1 - 1, hjb(T), put_mid)
    pairs(X0 + 2, X1 - 2, hjb(M), put_value)
    wait_recv(dy)
    transport((X0 + 3, X0 + half), half - 3)
    gi = strips(pl.ds(X0 + 3, nx - 6)) + [link(G.at[X0 + 3, rows], G.at[X1 + 3, rows], (-1, 0))]
    start(gi)

    wait_recv(hy)
    loop(X0, X1, lambda i: beyond_obstacles(1, i - X0, i))
    wait_recv(hx)

    def halo_obstacles(side, x, i):
        obstacles(side, x, i)
        beyond_obstacles(side, x, i)

    for j in range(2):
        halo_obstacles(0, nx - 2 + j, X0 - 2 + j)
    for j in range(3):
        halo_obstacles(2, j, X1 + j)

    wait_recv(tx + cx + second)
    ends(2, 1, hjb(T), put_mid)
    clear(M, 2, 2)
    ends(0, 2, hjb(M), put_value)
    for i in (X0 - 1, X1):
        put_halo(i, hjb(M)(i))
    clear(V, 1, 1)
    wait_recv(dx)
    transport((X0, X1 - 3), 3)

    gx = [field_link(G, d, 3, 0) for d in flat] + [field_link(G, d, 3, 3) for d in diagonals]
    gy = strips(pl.ds(X0, 3)) + strips(pl.ds(X1 - 3, 3))
    start(gy + gx)
    if whole:
        tell(2, token.at[0])

    def shifted(src):
        def f(i):
            v = src[i]
            return D4[i] * v - ((src[i + 1] + src[i - 1]) + (pltpu.roll(v, YE - 1, 0) + pltpu.roll(v, 1, 0))
                                + (z_up(v) + z_low(v)))
        return f

    R = M

    def residual(i):
        return (1.0 - SHIFT) * G[i] - shifted(G)(i)

    def into(dst):
        return lambda i, v: put(dst, i, v)

    def moments(i, sums):
        r, b = R[i, rows, :], B1[i, rows, :]
        full = Q[i]
        yu = pltpu.roll(full, YE - 1, 0)[:ny]
        q = full[:ny]
        image = D4[i, rows, :] * q - 2.0 * (Q[i + 1, rows, :] + yu + z_up(q))
        terms = (r * r, r * b, b * b, b * q, q * q, q * image)

        def fold(a):
            a = a.reshape(ny // 8, 8, nz).sum(axis=0)
            return sum(a[:, j:j + 128] for j in range(0, nz, 128))

        return tuple(s + fold(a) for s, a in zip(sums, terms))

    wait_recv(gi[:2])
    pairs(X0 + 4, X1 - 4, residual, into(R))
    wait_recv(gy)
    ends(-1, 4, residual, into(R))
    pairs(X0 + 2, X1 - 2, shifted(R), into(B1))
    pairs(X0 + 3, X1 - 3, shifted(B1), into(Q))

    def two(j, sums):
        return moments(X0 + 4 + 2 * j, moments(X0 + 3 + 2 * j, sums))

    zero = jnp.zeros((8, 128), jnp.float32)
    sums = lax.fori_loop(0, (nx - 8) // 2, two, (zero,) * 6)

    wait_recv(gx + gi[2:])
    if whole:
        hear(2, token.at[0])
        tell(4, token.at[1])
    ends(2, 1, residual, into(R))
    into(R)(X1 + 2, residual(X1 + 2))
    clear(R, 2, 3)
    ends(1, 2, shifted(R), into(B1))
    into(B1)(X1 + 1, shifted(R)(X1 + 1))
    clear(B1, 1, 2)
    ends(0, 3, shifted(B1), into(Q))
    into(Q)(X1, shifted(B1)(X1))
    clear(Q, 0, 1)

    def rest(j, sums):
        for k in (2 * j, 2 * j + 1):
            sums = moments(X0 + k + jnp.where(k >= 3, nx - 8, 0), sums)
        return sums

    sums = lax.fori_loop(0, 4, rest, sums)
    tile_row = lax.broadcasted_iota(jnp.int32, (8, 128), 0)
    tile = zero
    for k, s in enumerate(sums):
        tile = jnp.where(tile_row == k, jnp.sum(s, axis=0, keepdims=True), tile)
    tile = jnp.sum(tile, axis=1, keepdims=True)
    tile = jnp.sum(jnp.where(tile_row == lane[:8], tile, 0.0), axis=0, keepdims=True)

    def all_sum(slots, value, me, near, send, recv):
        slots[me] = value
        for d in near:
            pltpu.make_async_remote_copy(
                src_ref=slots.at[me], dst_ref=slots.at[me], send_sem=send.at[0], recv_sem=recv.at[0],
                device_id=peer(*d), device_id_type=MESH).start()
        area = slots.at[pl.ds(0, len(near))]
        every = pltpu.make_async_remote_copy(
            src_ref=area, dst_ref=area, send_sem=send.at[0], recv_sem=recv.at[0],
            device_id=peer(*near[0]), device_id_type=MESH)
        every.wait_recv()
        return [every], jnp.sum(slots[...], axis=0)

    if whole:
        hear(4, token.at[1])
        order = sorted(peers, key=lambda d: -min(d[1], nby - d[1]))
        ca, tile = all_sum(PA, tile, bx * nby + by, order, asend, arecv)
        cb = []
    else:
        ca, tile = all_sum(PA, tile, by, lines[:nby - 1], asend, arecv)
        cb, tile = all_sum(PB, tile, bx, lines[nby - 1:], bsend, brecv)
    nu = [jnp.broadcast_to(tile[:, k:k + 1], (1, 128)) for k in range(6)]

    def dot(p, q, s):
        total = 0.0
        for i, a in enumerate(p):
            for j, b in enumerate(q):
                total = total + a * b * nu[i + j + s]
        return total

    def energy(p):
        return SHIFT * dot(p, p, 0) + dot(p, p, 1)

    def step_of(rr, p):
        return jnp.clip(rr / energy(p), 1.0 / 17.0, 1.0)

    one = jnp.ones_like(nu[0])
    rr = nu[0]
    p, r = (one,), (one,)
    x = None
    for it in range(3):
        a = step_of(rr, p)
        x = [a * c for c in p] if x is None else [x[j] + a * p[j] if j < len(x) else a * p[j] for j in range(len(p))]
        if it == 2:
            break
        image = [SHIFT * c for c in p] + [jnp.zeros_like(one)]
        for j, c in enumerate(p):
            image[j + 1] = image[j + 1] + c
        r = tuple((r[j] if j < len(r) else 0.0) - a * image[j] for j in range(len(image)))
        new = jnp.maximum(dot(r, r, 0), 0.0)
        beta = new / rr
        p = tuple(r[j] + (beta * p[j] if j < len(p) else 0.0) for j in range(len(r)))
        rr = new
    x = [jnp.concatenate([c] * (nz // 128), axis=1) for c in x]

    def finish(i):
        s_out[i - X0] = G[i, rows, :] + x[0] * R[i, rows, :] + x[1] * B1[i, rows, :] + x[2] * Q[i, rows, :]

    loop(X0, X1, finish)

    wait_send(first + second + hx + hy + ty + cy + dy + tx + cx + dx + gi + gx + gy)
    for c in ca + cb:
        c.wait_send()


LINKS = 49


def write(v, s, v_out, s_out, sem):
    copies = [pltpu.make_async_copy(v, v_out, sem.at[0]), pltpu.make_async_copy(s, s_out, sem.at[1])]
    for c in copies:
        c.start()
    for c in copies:
        c.wait()


def per_device(nbx, nby, t, m, p, h):
    nx, ny, nz = t.shape
    slots = nbx * nby if nbx <= 4 and nby <= 8 else nby
    ext = pltpu.VMEM((nx + 2 * X0, ny + HALO, nz), jnp.float32)
    out = jax.ShapeDtypeStruct(t.shape, jnp.float32)
    v, s = pl.pallas_call(
        functools.partial(kernel, nbx, nby),
        out_shape=(out, out),
        in_specs=[pl.BlockSpec(memory_space=pl.ANY)] * 4,
        out_specs=(pl.BlockSpec(memory_space=pltpu.VMEM),) * 2,
        scratch_shapes=[ext] * 9 + [
            pltpu.VMEM((nx, ny, nz), jnp.float32),
            pltpu.VMEM((3, ny, nz), jnp.float32),
            pltpu.VMEM((3, 3, nx, ny), jnp.int32),
            pltpu.VMEM((slots, 1, 128), jnp.float32), pltpu.VMEM((nbx, 1, 128), jnp.float32),
            pltpu.SemaphoreType.DMA((LINKS,)), pltpu.SemaphoreType.DMA((LINKS,)),
            pltpu.SemaphoreType.DMA((1,)), pltpu.SemaphoreType.DMA((1,)),
            pltpu.SemaphoreType.DMA((1,)), pltpu.SemaphoreType.DMA((1,)),
            pltpu.SemaphoreType.DMA((4,)), pltpu.SemaphoreType.REGULAR((2,)),
        ],
        compiler_params=pltpu.CompilerParams(collective_id=0, has_side_effects=True, vmem_limit_bytes=VMEM_LIMIT),
        name="mean_field_step",
    )(*(pltpu.with_memory_space_constraint(a, pltpu.HBM) for a in (t, m, p, h)))
    return pl.pallas_call(
        write,
        out_shape=(out, out),
        in_specs=[pl.BlockSpec(memory_space=pltpu.VMEM)] * 2,
        out_specs=(pl.BlockSpec(memory_space=pl.ANY),) * 2,
        scratch_shapes=[pltpu.SemaphoreType.DMA((2,))],
        compiler_params=pltpu.CompilerParams(vmem_limit_bytes=4_000_000),
        name="write",
    )(v, s)


def solution(mesh):
    cells, plane = P_("bx", "by", None), P_("bx", "by")
    return jax.shard_map(
        functools.partial(per_device, mesh.shape["bx"], mesh.shape["by"]),
        mesh=mesh, in_specs=(cells, cells, cells, plane), out_specs=(cells, cells), check_vma=False)
```
